256 devices in a mesh: gx: 16 (over z, core), gy: 8 (over y_hi, x), ga: 2 (over y_lo).
Axes of the slice: x: 4, y: 4 (y_hi: 2, y_lo: 2; y = y_hi * 2 + y_lo), z: 8, core: 2. Of those that a mesh axis runs over, the one named last changes fastest.
Arguments:
- samples: bfloat16 [16, 128, 128, 512], P('ga', 'gx', 'gy'), parts along dimension 0, may hold values from -6 to 6
- model_prev: bfloat16 [16, 128, 128, 512], P('ga', 'gx', 'gy'), parts along dimension 0, may hold values from -6 to 6
- threshold: float32 [128, 128], P('gx', 'gy'), may hold values from 0.1 to 1
- support: int32 [128, 128, 256], P('gx', 'gy'), may hold values from 0 to 511
- sample_basis: bfloat16 [512, 64], replicated, may hold values from -0.25 to 0.25
- eval_basis: bfloat16 [64, 512], replicated, may hold values from -0.25 to 0.25
- transfer_x: bfloat16 [16, 16, 64, 64], replicated, may hold values from -0.1875 to 0.1875
- transfer_y: bfloat16 [8, 8, 64, 64], replicated, may hold values from -0.25 to 0.25
Outputs:
- model_next: float32 [16, 128, 128, 512], P('ga', 'gx', 'gy'), parts along dimension 0
- residual: bfloat16 [16, 128, 128, 512], P('ga', 'gx', 'gy'), parts along dimension 0
The draws below stay inside these ranges and needn't reach their ends.
There are 2 independent parts, one for each index of `ga`. The reference program is written for one: setup_inputs(seed, part) draws one part's arguments, and reference() takes and returns one part's arrays. A program takes and returns all parts, laid end to end along the dimension named above; an argument that names none is the same for every part. Nothing has to cross between parts.
All inputs are finite; a program needn't handle non-finite values.
Results may differ from the reference program's by a relative error of at most 0.015.
Values may be sent and summed in bfloat16 or wider, within the bound.
A program may use at most 64 MiB of HBM per device.

```python
import jax
import jax.numpy as jnp

G = 8
K = 64
LX = 8
LY = 16
SB = 512
RB = 512
NSUP = 256
BX = 128
BY = 128
N_GX = 16
N_GY = 8


def touch_ends(array, own_key, least, largest):
    index_at = [jax.random.randint(jax.random.fold_in(own_key, axis), (), 0, length) for axis, length in enumerate(array.shape)]
    widest = array.shape.index(max(array.shape))
    neighbour = index_at[:widest] + [(index_at[widest] + 1) % array.shape[widest]] + index_at[widest + 1:]
    return array.at[tuple(index_at)].set(least).at[tuple(neighbour)].set(largest)


def shard_levels(rng, shape, split, smallest, top_value):
    factor_of, own = 1.0, jax.random.fold_in(rng, 6)
    for position, shards_of in split:
        draws = jnp.exp(jax.random.uniform(jax.random.fold_in(own, position), (shards_of,), jnp.float32, smallest / len(split), top_value / len(split)))
        factor_of = factor_of * jnp.repeat(draws, shape[position] // shards_of).reshape([-1 if axis == position else 1 for axis in range(len(shape))])
    return factor_of


def bell_draw(stream_key, shape, deviation, reach, pieces=(), kind=jnp.bfloat16):
    drawn = deviation * jax.random.normal(stream_key, shape, jnp.float32)
    if pieces:
        drawn = drawn * shard_levels(stream_key, shape, pieces, -0.22, 0.18)
    return jnp.clip(drawn, -reach, reach).astype(kind)


def setup_inputs(seed: int = 0, part: int = 0) -> dict:
    key_list = jax.random.split(jax.random.key(seed), 9)
    own_keys = jax.random.split(jax.random.fold_in(key_list[8], part), 9)
    samples = bell_draw(own_keys[0], (G, BX, BY, SB), 1.0, 6.0, ((1, 16), (2, 8)))
    model_prev = bell_draw(own_keys[1], (G, BX, BY, RB), 1.0, 6.0, ((1, 16), (2, 8)))
    threshold = jnp.clip(0.1 + 0.9 * jax.random.uniform(key_list[2], (BX, BY), jnp.float32) ** shard_levels(key_list[2], (BX, BY), ((0, 16), (1, 8)), -0.2, 0.2), 0.1, 1.0)
    support = touch_ends(jax.random.randint(key_list[3], (BX, BY, NSUP), 0, RB), jax.random.fold_in(key_list[3], 1), 0, RB - 1).astype(jnp.int32)
    sample_basis = bell_draw(key_list[4], (SB, K), SB ** -0.5, 0.25)
    eval_basis = bell_draw(key_list[5], (K, RB), RB ** -0.5, 0.25)
    transfer_x = bell_draw(key_list[6], (N_GX, N_GX, K, K), (N_GX * K) ** -0.5, 0.1875)
    transfer_y = bell_draw(key_list[7], (N_GY, N_GY, K, K), (N_GY * K) ** -0.5, 0.25)
    return {"samples": samples, "model_prev": model_prev, "threshold": threshold, "support": support, "sample_basis": sample_basis, "eval_basis": eval_basis, "transfer_x": transfer_x, "transfer_y": transfer_y}


def level_mix_x(coeffs, tables):
    shaped = coeffs.astype(jnp.float32).reshape(G, N_GX, LX, BY, K)
    mixed = jnp.einsum('gslyk,askq->galyq', shaped, tables.astype(jnp.float32))
    return mixed.reshape(G, BX, BY, K)


def level_mix_y(coeffs, tables):
    shaped = coeffs.astype(jnp.float32).reshape(G, BX, N_GY, LY, K)
    mixed = jnp.einsum('gxsmk,askq->gxamq', shaped, tables.astype(jnp.float32))
    return mixed.reshape(G, BX, BY, K)


def reference(samples, model_prev, threshold, support, sample_basis, eval_basis, transfer_x, transfer_y):
    flipped_x = jnp.transpose(transfer_x, (1, 0, 3, 2))
    flipped_y = jnp.transpose(transfer_y, (1, 0, 3, 2))
    top = jnp.einsum('gxyr,kr->gxyk', model_prev.astype(jnp.float32), eval_basis.astype(jnp.float32)).astype(jnp.bfloat16)
    middle = level_mix_y(top, flipped_y).astype(jnp.bfloat16)
    low = level_mix_x(middle, flipped_x).astype(jnp.bfloat16)
    predicted = jnp.einsum('gxyk,tk->gxyt', low.astype(jnp.float32), sample_basis.astype(jnp.float32))
    residual = (samples.astype(jnp.float32) - predicted).astype(jnp.bfloat16)
    back_low = jnp.einsum('gxyt,tk->gxyk', residual.astype(jnp.float32), sample_basis.astype(jnp.float32)).astype(jnp.bfloat16)
    back_mid = level_mix_x(back_low, transfer_x).astype(jnp.bfloat16)
    back_top = level_mix_y(back_mid, transfer_y).astype(jnp.bfloat16)
    update = jnp.einsum('gxyk,kr->gxyr', back_top.astype(jnp.float32), eval_basis.astype(jnp.float32))
    stepped = model_prev.astype(jnp.float32) + update
    shrunk = jnp.sign(stepped) * jnp.maximum(jnp.abs(stepped) - threshold[None, :, :, None], 0.0)
    row_index = jnp.arange(BX, dtype=jnp.int32)[:, None, None]
    col_index = jnp.arange(BY, dtype=jnp.int32)[None, :, None]
    support_mask = jnp.zeros((BX, BY, RB), jnp.float32).at[row_index, col_index, support].set(1.0)
    return shrunk * support_mask[None], residual
```

```python
import functools

import jax
import jax.numpy as jnp
from jax import lax
from jax.experimental import pallas as pl
from jax.experimental.pallas import tpu as pltpu
from jax.sharding import PartitionSpec as P

BF = jnp.bfloat16
F32 = jnp.float32
MESH = pl.DeviceIdType.MESH
NX, NY = 16, 8
LAST = (((1,), (1,)), ((), ()))
PLAIN = (((1,), (0,)), ((), ()))


def dot(a, b, dims=PLAIN):
    return lax.dot_general(a, b, dims, preferred_element_type=F32)


def halves(u, v):
    return (
        jnp.concatenate([u[:, :64], v[:, :64]], axis=1),
        jnp.concatenate([u[:, 64:], v[:, 64:]], axis=1),
    )


def kernel(
    samples, model, thr, sup, sb, eb, tx, ty,
    out_model, out_res,
    m_v, s_v, tx_v, ty_v, bx, by, sb_v, eb_v, sl, sh, ea, ez, sup_v, supt, bits, thr_v, teff,
    res_v, om_v,
    s1, s2, s3, s4, s5, s6, r1, r2, r3, r4, r5, r6,
    in_sem, out_sem, send_sem, recv_sem,
):
    gx, gy = lax.axis_index("gx"), lax.axis_index("gy")
    half, owner = lax.rem(gx, 2), gx // 2
    own = owner == gy

    loads = [
        (model, m_v), (eb, eb_v), (ty, ty_v), (tx, tx_v),
        (sup, sup_v), (thr, thr_v), (sb, sb_v), (samples, s_v),
    ]
    copies = [
        pltpu.make_async_copy(src, dst, in_sem.at[i]) for i, (src, dst) in enumerate(loads)
    ]
    for copy in copies:
        copy.start()

    barrier = pltpu.get_barrier_semaphore()

    def greet(x, y):
        pl.semaphore_signal(barrier, inc=1, device_id={"gx": x, "gy": y}, device_id_type=MESH)

    @pl.loop(1, NX)
    def _(d):
        greet(lax.rem(gx + d, NX), gy)

    @pl.loop(1, NY)
    def _(d):
        greet(gx, lax.rem(gy + d, NY))

    @pl.loop(0, NX)
    def _(d):
        @pl.when(jnp.logical_not(jnp.logical_and(own, d == gx)))
        def _():
            greet(d, owner)

    @pl.loop(0, NX)
    def _(d):
        x, y = gy * 2 + lax.rem(d, 2), d // 2

        @pl.when(jnp.logical_not(jnp.logical_and(own, x == gx) & (y == gy)))
        def _():
            greet(x, y)

    copies[1].wait()
    copies[0].wait()
    e = eb_v[...]
    ea[...] = jnp.concatenate([e, jnp.zeros_like(e)], axis=0)
    ez[...] = jnp.concatenate([jnp.zeros_like(e), e], axis=0)
    for b in range(0, NY, 4):
        rows_a = jnp.concatenate([m_v[pl.ds(128 * j, 64), :] for j in range(b, b + 4)], axis=0)
        rows_b = jnp.concatenate([m_v[pl.ds(128 * j + 64, 64), :] for j in range(b, b + 4)], axis=0)
        packed = dot(rows_a, ea[...], LAST) + dot(rows_b, ez[...], LAST)
        s1[b : b + 4] = packed.astype(BF).reshape(4, 64, 128)

    pl.semaphore_wait(barrier, jnp.where(own, 52, 54))

    def along_y(i, src, dst):
        @pl.loop(1, NY)
        def _(d):
            j = lax.rem(gy + d, NY)
            pltpu.make_async_remote_copy(
                src_ref=src.at[j], dst_ref=dst.at[gy], send_sem=send_sem.at[i],
                recv_sem=recv_sem.at[i], device_id={"gy": j}, device_id_type=MESH,
            ).start()

        pltpu.make_async_copy(src.at[gy], dst.at[gy], recv_sem.at[i]).start()

    def along_x(i, src, dst):
        @pl.loop(1, NX)
        def _(d):
            j = lax.rem(gx + d, NX)
            pltpu.make_async_remote_copy(
                src_ref=src.at[j], dst_ref=dst.at[gx], send_sem=send_sem.at[i],
                recv_sem=recv_sem.at[i], device_id={"gx": j}, device_id_type=MESH,
            ).start()

        pltpu.make_async_copy(src.at[gx], dst.at[gx], recv_sem.at[i]).start()

    def across(i, src, dst, slot, target):
        @pl.loop(0, NX)
        def _(d):
            j = lax.rem(gx + d, NX)
            x, y = target(j)
            mine = jnp.logical_and(x == gx, y == gy)

            @pl.when(jnp.logical_not(mine))
            def _():
                pltpu.make_async_remote_copy(
                    src_ref=src.at[j], dst_ref=dst.at[slot], send_sem=send_sem.at[i],
                    recv_sem=recv_sem.at[i], device_id={"gx": x, "gy": y}, device_id_type=MESH,
                ).start()

            @pl.when(mine)
            def _():
                pltpu.make_async_copy(src.at[j], dst.at[slot], recv_sem.at[i]).start()

    def arrive(i, dst):
        pltpu.make_async_copy(dst, dst, recv_sem.at[i]).wait()

    along_y(0, s1, r1)

    copies[2].wait()
    for p in range(NY // 2):
        by[:, 128 * p : 128 * p + 128] = jnp.concatenate([ty_v[2 * p], ty_v[2 * p + 1]], axis=1)
    arrive(0, r1)
    lows, highs = zip(*[halves(r1[2 * p], r1[2 * p + 1]) for p in range(NY // 2)])
    rows = jnp.concatenate(
        [jnp.concatenate(lows, axis=1), jnp.concatenate(highs, axis=1)], axis=0
    )
    mixed = dot(rows, by[...], LAST).astype(BF)
    for p in range(NY // 2):
        part = mixed[:, 128 * p : 128 * p + 128]
        for h in range(2):
            even, odd = halves(part[64 * h : 64 * h + 32], part[64 * h + 32 : 64 * h + 64])
            s2[4 * p + h] = even
            s2[4 * p + 2 + h] = odd
    along_x(1, s2, r2)

    copies[3].wait()
    for p in range(NX // 2):
        bx[:, 128 * p : 128 * p + 128] = jnp.concatenate([tx_v[2 * p], tx_v[2 * p + 1]], axis=1)

    def gathered(r):
        lows, highs = zip(*[halves(r[2 * p], r[2 * p + 1]) for p in range(NX // 2)])
        return jnp.concatenate(
            [jnp.concatenate(lows, axis=1), jnp.concatenate(highs, axis=1)], axis=0
        )

    def spread(mixed, s):
        for p in range(NX // 2):
            part = mixed[:, 128 * p : 128 * p + 128]
            s[2 * p], s[2 * p + 1] = halves(part[:32], part[32:])

    arrive(1, r2)
    spread(dot(gathered(r2), bx[...], LAST).astype(BF), s3)
    across(2, s3, r3, gy * 2 + half, lambda j: (j, owner))

    copies[4].wait()
    copies[5].wait()
    copies[6].wait()
    base = sb_v[...]
    sl[...] = jnp.concatenate([base, jnp.zeros_like(base)], axis=0)
    sh[...] = jnp.concatenate([jnp.zeros_like(base), base], axis=0)
    supt[...] = jnp.transpose(sup_v[...])
    words = lax.broadcasted_iota(jnp.int32, (16, 128), 0)

    def gather_bits(i, acc):
        tile = supt[pl.ds(pl.multiple_of(i * 8, 8), 8), :]
        word = lax.shift_right_logical(tile, 5)
        bit = lax.shift_left(jnp.ones_like(tile), tile & 31)
        for n in range(8):
            hit = words == word[n : n + 1, :]
            acc = acc | jnp.where(hit, bit[n : n + 1, :], 0)
        return acc

    bits[...] = lax.fori_loop(0, 32, gather_bits, jnp.zeros((16, 128), jnp.int32))
    place = lax.broadcasted_iota(jnp.int32, (32, 128), 0)
    diagonal = lax.broadcasted_iota(jnp.int32, (16, 16), 0) == lax.broadcasted_iota(
        jnp.int32, (16, 16), 1
    )
    columns = [
        jnp.sum(jnp.where(diagonal, thr_v[l : l + 1, :], 0.0), axis=1, keepdims=True)
        for l in range(8)
    ]
    column = jnp.concatenate(columns, axis=0)
    for c in range(4):
        stacked = jnp.concatenate(
            [lax.shift_right_logical(jnp.broadcast_to(bits[4 * c + w : 4 * c + w + 1, :], (32, 128)), place) & 1
             for w in range(4)],
            axis=0,
        )
        kept = jnp.transpose(stacked.astype(F32))
        teff[:, 128 * c : 128 * c + 128] = jnp.where(kept > 0.0, column, jnp.inf)
    copies[7].wait()

    arrive(2, r3)
    for c in range(4):
        low = r3[4 * c : 4 * c + 4].reshape(128, 128)
        total = None
        for w, basis in enumerate((sl, sh)):
            predicted = dot(low, basis[...])
            held = s_v[4 * c : 4 * c + 4, w].reshape(128, 512).astype(F32)
            res = (held - predicted).astype(BF)
            res_v[4 * c : 4 * c + 4, w] = res.reshape(4, 32, 512)
            back = dot(res, basis[...], LAST)
            total = back if total is None else total + back
        s4[4 * c : 4 * c + 4] = total.astype(BF).reshape(4, 32, 128)
    across(3, s4, r4, gx, lambda j: (gy * 2 + lax.rem(j, 2), j // 2))
    res_out = pltpu.make_async_copy(res_v, out_res, out_sem.at[0])
    res_out.start()

    arrive(3, r4)
    spread(dot(gathered(r4), bx[...]).astype(BF), s5)
    along_x(4, s5, r5)

    arrive(4, r5)
    blocks = []
    for h in range(2):
        lows, highs = zip(*[halves(r5[4 * p + h], r5[4 * p + 2 + h]) for p in range(NY // 2)])
        blocks += [jnp.concatenate(lows, axis=1), jnp.concatenate(highs, axis=1)]
    mixed = dot(jnp.concatenate(blocks, axis=0), by[...]).astype(BF)
    for p in range(NY // 2):
        part = mixed[:, 128 * p : 128 * p + 128]
        s6[2 * p], s6[2 * p + 1] = halves(part[:64], part[64:])
    along_y(5, s6, r6)

    arrive(5, r6)
    for b in range(NY):
        back_top = r6[b]
        for w, basis in enumerate((ea, ez)):
            v = m_v[pl.ds(128 * b + 64 * w, 64), :].astype(F32) + dot(back_top, basis[...])
            t = teff[64 * w : 64 * w + 64, :]
            om_v[pl.ds(128 * b + 64 * w, 64), :] = v - jnp.minimum(jnp.maximum(v, -t), t)
    model_out = pltpu.make_async_copy(om_v, out_model, out_sem.at[1])
    model_out.start()

    for i, (src, per) in enumerate(((s1, 7), (s2, 15), (s3, 15), (s4, 15), (s5, 15), (s6, 7))):
        sent = src.at[pl.ds(0, per)]
        pltpu.make_async_copy(sent, sent, send_sem.at[i]).wait()

    @pl.when(jnp.logical_not(own))
    def _():
        for i, src in ((2, s3), (3, s4)):
            pltpu.make_async_copy(src.at[0], src.at[0], send_sem.at[i]).wait()

    res_out.wait()
    model_out.wait()


def on_device(
    samples, model_prev, threshold, support, sample_basis, eval_basis, transfer_x, transfer_y
):
    hbm = pl.BlockSpec(memory_space=pltpu.HBM)
    wide = pltpu.VMEM((8, 64, 128), BF)
    thin = pltpu.VMEM((16, 32, 128), BF)
    model_next, residual = pl.pallas_call(
        kernel,
        out_shape=(
            jax.ShapeDtypeStruct((1024, 512), F32),
            jax.ShapeDtypeStruct((16, 2, 32, 512), BF),
        ),
        in_specs=[hbm] * 8,
        out_specs=(hbm, hbm),
        scratch_shapes=[
            pltpu.VMEM((1024, 512), BF),
            pltpu.VMEM((16, 2, 32, 512), BF),
            pltpu.VMEM((16, 1024, 64), BF),
            pltpu.VMEM((8, 512, 64), BF),
            pltpu.VMEM((1024, 1024), BF),
            pltpu.VMEM((512, 512), BF),
            pltpu.VMEM((64, 512), BF),
            pltpu.VMEM((64, 512), BF),
            pltpu.VMEM((128, 512), BF),
            pltpu.VMEM((128, 512), BF),
            pltpu.VMEM((128, 512), BF),
            pltpu.VMEM((128, 512), BF),
            pltpu.VMEM((128, 256), jnp.int32),
            pltpu.VMEM((256, 128), jnp.int32),
            pltpu.VMEM((16, 128), jnp.int32),
            pltpu.VMEM((8, 16), F32),
            pltpu.VMEM((128, 512), F32),
            pltpu.VMEM((16, 2, 32, 512), BF),
            pltpu.VMEM((1024, 512), F32),
            wide, thin, thin, thin, thin, wide,
            wide, thin, thin, thin, thin, wide,
            pltpu.SemaphoreType.DMA((8,)),
            pltpu.SemaphoreType.DMA((2,)),
            pltpu.SemaphoreType.DMA((6,)),
            pltpu.SemaphoreType.DMA((6,)),
        ],
        compiler_params=pltpu.CompilerParams(
            collective_id=0, has_side_effects=True, vmem_limit_bytes=58 * 2**20
        ),
    )(
        samples.reshape(16, 2, 32, 512),
        model_prev.reshape(1024, 512),
        threshold,
        support.reshape(128, 256),
        sample_basis.T,
        eval_basis,
        transfer_x.reshape(16, 1024, 64),
        transfer_y.reshape(8, 512, 64),
    )
    return model_next.reshape(8, 8, 16, 512), residual.reshape(8, 8, 16, 512)


def solution(mesh):
    return jax.shard_map(
        on_device,
        mesh=mesh,
        in_specs=(
            P("ga", "gx", "gy", None),
            P("ga", "gx", "gy", None),
            P("gx", "gy"),
            P("gx", "gy", None),
            P(),
            P(),
            P(),
            P(),
        ),
        out_specs=(P("ga", "gx", "gy", None), P("ga", "gx", "gy", None)),
        check_vma=False,
    )
```

```python
import jax
import jax.numpy as jnp
from jax import lax
from jax.experimental import pallas as pl
from jax.experimental.pallas import tpu as pltpu
from jax.sharding import PartitionSpec as P

BF = jnp.bfloat16
F32 = jnp.float32
MESH = pl.DeviceIdType.MESH
NX, NY = 16, 8
N = NX * NY
LAST = (((1,), (1,)), ((), ()))
PLAIN = (((1,), (0,)), ((), ()))


def dot(a, b, dims=PLAIN):
    return lax.dot_general(a, b, dims, preferred_element_type=F32)


def kernel(
    samples, model, thr, sup, sb, eb, tx, ty,
    om_v, res_v,
    m_v, s_v, tx_v, ty_v, bx, by, sb_v, eb_v, e_lo, s_lo, e_hi, s_hi, gram, sup_v, supt, bits, thr_v, teff,
    top_out, top_in, smp_out, smp_in, low_out, low_home, back_out, back_home,
    in_sem, send_sem, recv_sem,
):
    gx, gy = lax.axis_index("gx"), lax.axis_index("gy")
    me = gx * NY + gy
    left = lax.broadcasted_iota(jnp.int32, (8, 128), 1) < 64
    straight = left == (lax.broadcasted_iota(jnp.int32, (8, 128), 0) < 4)

    def swap(u):
        return pltpu.roll(u, 64, 1)

    def turn(u):
        return jnp.where(straight, u, pltpu.roll(swap(u), 4, 0))

    loads = [
        (model, m_v), (eb, eb_v), (sb, sb_v), (samples, s_v),
        (ty, ty_v), (tx, tx_v), (sup, sup_v), (thr, thr_v),
    ]
    copies = [
        pltpu.make_async_copy(src, dst, in_sem.at[i]) for i, (src, dst) in enumerate(loads)
    ]
    for copy in copies[:4]:
        copy.start()

    def plane(i):
        away = (i + 1) // 2
        return lax.rem(gx // 2 + 4 + jnp.where(lax.rem(i, 2) == 0, away, 8 - away), 8)

    columns_y = [lax.rem(gy + d, NY) for d in (6, 2, 5, 3, 4, 7, 1)] + [gy]

    def each_partner(act):
        @pl.loop(0, NX - 1)
        def _(i):
            away = (i + 1) // 2
            x = lax.rem(gx + 8 + jnp.where(lax.rem(i, 2) == 0, away, NX - away), NX)
            for y in columns_y:
                act(x, y)

        for y in columns_y[:-1]:
            act(gx, y)

    barrier = pltpu.get_barrier_semaphore()

    each_partner(
        lambda x, y: pl.semaphore_signal(
            barrier, inc=1, device_id={"gx": x, "gy": y}, device_id_type=MESH
        )
    )

    copies[1].wait()
    e = eb_v[...]
    zero = jnp.zeros_like(e)
    e_lo[...] = jnp.concatenate([e, zero], axis=0)
    e_hi[...] = jnp.concatenate([zero, e], axis=0)
    copies[2].wait()
    base = sb_v[...]
    s_lo[...] = jnp.concatenate([base, zero], axis=0)
    s_hi[...] = jnp.concatenate([zero, base], axis=0)
    copies[0].wait()
    for copy in copies[4:]:
        copy.start()
    top_out[...] = (dot(m_v[:512], e_lo[...], LAST) + dot(m_v[512:], e_hi[...], LAST)).astype(BF)

    pl.semaphore_wait(barrier, N - 1)

    def slot(i):
        return pl.ds(pl.multiple_of(i * 4, 4), 4)

    def along(x, y):
        return x * NY + y

    def crossed(x, y):
        return y * NX + x

    def exchange(i, src, at, dst, here, arrived):
        def send(x, y):
            pltpu.make_async_remote_copy(
                src_ref=src.at[slot(at(x, y))], dst_ref=dst.at[slot(here)],
                send_sem=send_sem.at[i], recv_sem=arrived,
                device_id={"gx": x, "gy": y}, device_id_type=MESH,
            ).start()

        each_partner(send)
        pltpu.make_async_copy(src.at[slot(at(gx, gy))], dst.at[slot(here)], arrived).start()

    def arrive(dst, arrived):
        pltpu.make_async_copy(dst, dst, arrived).wait()

    exchange(0, top_out, along, top_in, crossed(gx, gy), recv_sem.at[8])

    copies[3].wait()
    smp_out[...] = (dot(s_v[:512], s_lo[...], LAST) + dot(s_v[512:], s_hi[...], LAST)).astype(BF)
    exchange(1, smp_out, along, smp_in, me, recv_sem.at[9])

    copies[4].wait()
    for p in range(NY // 2):
        by[:, 128 * p : 128 * p + 128] = jnp.concatenate([ty_v[2 * p], ty_v[2 * p + 1]], axis=1)
    copies[5].wait()
    for p in range(NX // 2):
        bx[:, 128 * p : 128 * p + 128] = jnp.concatenate([tx_v[2 * p], tx_v[2 * p + 1]], axis=1)

    block = dot(s_lo[...], s_lo[...], LAST) + dot(s_hi[...], s_hi[...], LAST)
    major = block.astype(BF)
    gram[:128] = major
    gram[128:] = (block - major.astype(F32)).astype(BF)

    copies[6].wait()
    copies[7].wait()
    supt[...] = jnp.transpose(sup_v[...])
    words = lax.broadcasted_iota(jnp.int32, (16, 128), 0)

    def gather_bits(i, acc):
        tile = supt[pl.ds(pl.multiple_of(i * 8, 8), 8), :]
        word = lax.shift_right_logical(tile, 5)
        bit = lax.shift_left(jnp.ones_like(tile), tile & 31)
        for n in range(8):
            hit = words == word[n : n + 1, :]
            acc = acc | jnp.where(hit, bit[n : n + 1, :], 0)
        return acc

    bits[...] = lax.fori_loop(0, 32, gather_bits, jnp.zeros((16, 128), jnp.int32))
    place = lax.broadcasted_iota(jnp.int32, (32, 128), 0)
    diagonal = lax.broadcasted_iota(jnp.int32, (16, 16), 0) == lax.broadcasted_iota(
        jnp.int32, (16, 16), 1
    )
    columns = [
        jnp.sum(jnp.where(diagonal, thr_v[l : l + 1, :], 0.0), axis=1, keepdims=True)
        for l in range(8)
    ]
    column = jnp.concatenate(columns, axis=0)
    for c in range(4):
        stacked = jnp.concatenate(
            [lax.shift_right_logical(jnp.broadcast_to(bits[4 * c + w : 4 * c + w + 1, :], (32, 128)), place) & 1
             for w in range(4)],
            axis=0,
        )
        kept = jnp.transpose(stacked.astype(F32))
        teff[:, 128 * c : 128 * c + 128] = jnp.where(kept > 0.0, column, jnp.inf)

    def tile(ref, i):
        return ref[pl.ds(4 * i, 8), :].astype(F32)

    def assembled(parts):
        return jnp.concatenate([jnp.concatenate(row, axis=1) for row in parts], axis=0)

    def paired(ref, i, k):
        u, v = tile(ref, i), tile(ref, k)
        return jnp.where(left, u, swap(v)), jnp.where(left, swap(u), v)

    def part(u, i, k):
        return u[8 * i : 8 * i + 8, 128 * k : 128 * k + 128]

    HX, HY = NX // 2, NY // 2
    arrive(top_in, recv_sem.at[8])
    parts = [[None] * HY for _ in range(NX)]
    for q in range(HX):
        for p in range(HY):
            parts[q][p], parts[HX + q][p] = paired(
                top_in, crossed(2 * q, 2 * p), crossed(2 * q, 2 * p + 1)
            )
    middle = dot(assembled(parts).astype(BF), by[...], LAST)
    low = dot(
        assembled(
            [[turn(part(middle, HX * w + q, p)) for q in range(HX)] for w in range(2) for p in range(HY)]
        ).astype(BF),
        bx[...],
        LAST,
    )
    for q in range(HX):
        for p in range(HY):
            u, v = part(low, p, q), part(low, HY + p, q)
            low_out[pl.ds(4 * along(2 * q, 2 * p), 8), :] = jnp.where(left, u, swap(v)).astype(BF)
            low_out[pl.ds(4 * along(2 * q + 1, 2 * p), 8), :] = jnp.where(left, swap(u), v).astype(BF)
    exchange(2, low_out, along, low_home, me, recv_sem.at[10])

    low_bf = low.astype(BF)
    stacked = jnp.concatenate([low_bf[:, 128 * q : 128 * q + 128] for q in range(HX)], axis=0)
    taken = dot(stacked, gram[:128]) + dot(stacked, gram[128:])
    arrive(smp_in, recv_sem.at[9])
    parts = [[None] * HX for _ in range(NY)]
    for q in range(HX):
        for p in range(HY):
            u, v = paired(smp_in, along(2 * q, 2 * p), along(2 * q + 1, 2 * p))
            parts[p][q] = u - part(taken, NY * q + p, 0)
            parts[HY + p][q] = v - part(taken, NY * q + HY + p, 0)
    back_mid = dot(assembled(parts).astype(BF), bx[...])
    back_top = dot(
        assembled(
            [[turn(part(back_mid, HY * w + p, q)) for p in range(HY)] for w in range(2) for q in range(HX)]
        ).astype(BF),
        by[...],
    )
    for q in range(HX):
        for p in range(HY):
            u, v = part(back_top, q, p), part(back_top, HX + q, p)
            back_out[pl.ds(4 * crossed(2 * q, 2 * p), 8), :] = jnp.where(left, u, swap(v)).astype(BF)
            back_out[pl.ds(4 * crossed(2 * q, 2 * p + 1), 8), :] = jnp.where(left, swap(u), v).astype(BF)
    exchange(3, back_out, crossed, back_home, me, recv_sem.at[gx // 2])

    arrive(low_home, recv_sem.at[10])
    for w, basis in enumerate((s_lo, s_hi)):
        for b in range(4):
            block = pl.ds(512 * w + 128 * b, 128)
            predicted = dot(low_home[pl.ds(128 * b, 128), :], basis[...])
            res_v[block, :] = (s_v[block, :].astype(F32) - predicted).astype(BF)

    @pl.loop(0, 8)
    def _(i):
        z = plane(i)
        rows = pl.ds(pl.multiple_of(64 * z, 64), 64)
        arrive(back_home.at[rows], recv_sem.at[z])
        home = back_home[rows, :]
        t = teff[pl.ds(pl.multiple_of(64 * lax.rem(z, 2), 64), 64), :]
        for w, basis in enumerate((e_lo, e_hi)):
            block = pl.ds(pl.multiple_of(512 * w + 64 * z, 64), 64)
            v = m_v[block, :].astype(F32) + dot(home, basis[...])
            om_v[block, :] = v - jnp.minimum(jnp.maximum(v, -t), t)

    for i, src in enumerate((top_out, smp_out, low_out, back_out)):
        sent = src.at[pl.ds(0, 4 * (N - 1))]
        pltpu.make_async_copy(sent, sent, send_sem.at[i]).wait()


def on_device(
    samples, model_prev, threshold, support, sample_basis, eval_basis, transfer_x, transfer_y
):
    hbm = pl.BlockSpec(memory_space=pltpu.HBM)
    traffic = pltpu.VMEM((4 * N, 128), BF)
    model_next, residual = pl.pallas_call(
        kernel,
        out_shape=(
            jax.ShapeDtypeStruct((1024, 512), F32),
            jax.ShapeDtypeStruct((1024, 512), BF),
        ),
        in_specs=[hbm] * 8,
        out_specs=(pl.BlockSpec(memory_space=pltpu.VMEM),) * 2,
        scratch_shapes=[
            pltpu.VMEM((1024, 512), BF),
            pltpu.VMEM((1024, 512), BF),
            pltpu.VMEM((16, 1024, 64), BF),
            pltpu.VMEM((8, 512, 64), BF),
            pltpu.VMEM((1024, 1024), BF),
            pltpu.VMEM((512, 512), BF),
            pltpu.VMEM((64, 512), BF),
            pltpu.VMEM((64, 512), BF),
            pltpu.VMEM((128, 512), BF),
            pltpu.VMEM((128, 512), BF),
            pltpu.VMEM((128, 512), BF),
            pltpu.VMEM((128, 512), BF),
            pltpu.VMEM((256, 128), BF),
            pltpu.VMEM((128, 256), jnp.int32),
            pltpu.VMEM((256, 128), jnp.int32),
            pltpu.VMEM((16, 128), jnp.int32),
            pltpu.VMEM((8, 16), F32),
            pltpu.VMEM((128, 512), F32),
            traffic, traffic, traffic, traffic, traffic, traffic, traffic, traffic,
            pltpu.SemaphoreType.DMA((8,)),
            pltpu.SemaphoreType.DMA((4,)),
            pltpu.SemaphoreType.DMA((11,)),
        ],
        compiler_params=pltpu.CompilerParams(
            collective_id=0, has_side_effects=True, vmem_limit_bytes=30 * 2**20
        ),
    )(
        *[pltpu.with_memory_space_constraint(v, pltpu.HBM) for v in (
        samples.reshape(1024, 512),
        model_prev.reshape(1024, 512),
        threshold,
        support.reshape(128, 256),
        sample_basis.T,
        eval_basis,
        transfer_x.reshape(16, 1024, 64),
        transfer_y.reshape(8, 512, 64),
    )])
    return model_next.reshape(8, 8, 16, 512), residual.reshape(8, 8, 16, 512)


def solution(mesh):
    return jax.shard_map(
        on_device,
        mesh=mesh,
        in_specs=(
            P("ga", "gx", "gy", None),
            P("ga", "gx", "gy", None),
            P("gx", "gy"),
            P("gx", "gy", None),
            P(),
            P(),
            P(),
            P(),
        ),
        out_specs=(P("ga", "gx", "gy", None), P("ga", "gx", "gy", None)),
        check_vma=False,
    )
```

```python
import jax
import jax.numpy as jnp
from jax import lax
from jax.experimental import pallas as pl
from jax.experimental.pallas import tpu as pltpu
from jax.sharding import PartitionSpec as P

BF = jnp.bfloat16
F32 = jnp.float32
MESH = pl.DeviceIdType.MESH
NX, NY = 16, 8
N = NX * NY
LAST = (((1,), (1,)), ((), ()))
PLAIN = (((1,), (0,)), ((), ()))


def dot(a, b, dims=PLAIN):
    return lax.dot_general(a, b, dims, preferred_element_type=F32)


def kernel(
    samples, model, thr, sup, sb, eb, tx, ty,
    om_v, res_v,
    m_v, s_v, tx_v, ty_v, bx, by, sb_v, eb_v, e_lo, s_lo, e_hi, s_hi, gram, sup_v, supt, bits, thr_v, teff,
    top_out, top_in, smp_out, smp_in, low_out, low_home, back_out, back_home,
    in_sem, send_sem, recv_sem,
):
    gx, gy = lax.axis_index("gx"), lax.axis_index("gy")
    me = gx * NY + gy
    left = lax.broadcasted_iota(jnp.int32, (8, 128), 1) < 64
    straight = left == (lax.broadcasted_iota(jnp.int32, (8, 128), 0) < 4)

    def swap(u):
        return pltpu.roll(u, 64, 1)

    def turn(u):
        return jnp.where(straight, u, pltpu.roll(swap(u), 4, 0))

    loads = [
        (model, m_v), (eb, eb_v), (sb, sb_v), (samples, s_v),
        (ty, ty_v), (tx, tx_v), (sup, sup_v), (thr, thr_v),
    ]
    copies = [
        pltpu.make_async_copy(src, dst, in_sem.at[i]) for i, (src, dst) in enumerate(loads)
    ]

    def plane(i):
        away = (i + 1) // 2
        return lax.rem(gx // 2 + 4 + jnp.where(lax.rem(i, 2) == 0, away, 8 - away), 8)

    columns_y = [lax.rem(gy + d, NY) for d in (6, 2, 5, 3, 4, 7, 1)] + [gy]

    def each_partner(act):
        @pl.loop(0, NX - 1)
        def _(i):
            away = (i + 1) // 2
            x = lax.rem(gx + 8 + jnp.where(lax.rem(i, 2) == 0, away, NX - away), NX)
            for y in columns_y:
                act(x, y)

        for y in columns_y[:-1]:
            act(gx, y)

    barrier = pltpu.get_barrier_semaphore()

    each_partner(
        lambda x, y: pl.semaphore_signal(
            barrier, inc=1, device_id={"gx": x, "gy": y}, device_id_type=MESH
        )
    )
    for copy in copies:
        copy.start()

    copies[1].wait()
    e = eb_v[...]
    zero = jnp.zeros_like(e)
    e_lo[...] = jnp.concatenate([e, zero], axis=0)
    e_hi[...] = jnp.concatenate([zero, e], axis=0)
    copies[2].wait()
    base = sb_v[...]
    s_lo[...] = jnp.concatenate([base, zero], axis=0)
    s_hi[...] = jnp.concatenate([zero, base], axis=0)
    copies[0].wait()
    top_out[...] = (dot(m_v[:512], e_lo[...], LAST) + dot(m_v[512:], e_hi[...], LAST)).astype(BF)

    pl.semaphore_wait(barrier, N - 1)

    def slot(i):
        return pl.ds(pl.multiple_of(i * 4, 4), 4)

    def along(x, y):
        return x * NY + y

    def crossed(x, y):
        return y * NX + x

    def exchange(i, src, at, dst, here, arrived):
        def send(x, y):
            pltpu.make_async_remote_copy(
                src_ref=src.at[slot(at(x, y))], dst_ref=dst.at[slot(here)],
                send_sem=send_sem.at[i], recv_sem=arrived,
                device_id={"gx": x, "gy": y}, device_id_type=MESH,
            ).start()

        each_partner(send)
        pltpu.make_async_copy(src.at[slot(at(gx, gy))], dst.at[slot(here)], arrived).start()

    def arrive(dst, arrived):
        pltpu.make_async_copy(dst, dst, arrived).wait()

    exchange(0, top_out, along, top_in, crossed(gx, gy), recv_sem.at[8])

    copies[3].wait()
    smp_out[...] = (dot(s_v[:512], s_lo[...], LAST) + dot(s_v[512:], s_hi[...], LAST)).astype(BF)
    exchange(1, smp_out, along, smp_in, me, recv_sem.at[9])

    block = dot(s_lo[...], s_lo[...], LAST) + dot(s_hi[...], s_hi[...], LAST)
    major = block.astype(BF)
    gram[:128] = major
    gram[128:] = (block - major.astype(F32)).astype(BF)

    copies[4].wait()
    for p in range(NY // 2):
        by[:, 128 * p : 128 * p + 128] = jnp.concatenate([ty_v[2 * p], ty_v[2 * p + 1]], axis=1)
    copies[5].wait()
    for p in range(NX // 2):
        bx[:, 128 * p : 128 * p + 128] = jnp.concatenate([tx_v[2 * p], tx_v[2 * p + 1]], axis=1)

    def tile(ref, i):
        return ref[pl.ds(4 * i, 8), :].astype(F32)

    def assembled(parts):
        return jnp.concatenate([jnp.concatenate(row, axis=1) for row in parts], axis=0)

    def paired(ref, i, k):
        u, v = tile(ref, i), tile(ref, k)
        return jnp.where(left, u, swap(v)), jnp.where(left, swap(u), v)

    def part(u, i, k):
        return u[8 * i : 8 * i + 8, 128 * k : 128 * k + 128]

    HX, HY = NX // 2, NY // 2
    arrive(top_in, recv_sem.at[8])
    parts = [[None] * HY for _ in range(NX)]
    for q in range(HX):
        for p in range(HY):
            parts[q][p], parts[HX + q][p] = paired(
                top_in, crossed(2 * q, 2 * p), crossed(2 * q, 2 * p + 1)
            )
    middle = dot(assembled(parts).astype(BF), by[...], LAST)
    low = dot(
        assembled(
            [[turn(part(middle, HX * w + q, p)) for q in range(HX)] for w in range(2) for p in range(HY)]
        ).astype(BF),
        bx[...],
        LAST,
    )
    for q in range(HX):
        for p in range(HY):
            u, v = part(low, p, q), part(low, HY + p, q)
            low_out[pl.ds(4 * along(2 * q, 2 * p), 8), :] = jnp.where(left, u, swap(v)).astype(BF)
            low_out[pl.ds(4 * along(2 * q + 1, 2 * p), 8), :] = jnp.where(left, swap(u), v).astype(BF)
    exchange(2, low_out, along, low_home, me, recv_sem.at[10])

    low_bf = low.astype(BF)
    stacked = jnp.concatenate([low_bf[:, 128 * q : 128 * q + 128] for q in range(HX)], axis=0)
    taken = dot(stacked, gram[:128]) + dot(stacked, gram[128:])
    arrive(smp_in, recv_sem.at[9])
    parts = [[None] * HX for _ in range(NY)]
    for q in range(HX):
        for p in range(HY):
            u, v = paired(smp_in, along(2 * q, 2 * p), along(2 * q + 1, 2 * p))
            parts[p][q] = u - part(taken, NY * q + p, 0)
            parts[HY + p][q] = v - part(taken, NY * q + HY + p, 0)
    back_mid = dot(assembled(parts).astype(BF), bx[...])
    back_top = dot(
        assembled(
            [[turn(part(back_mid, HY * w + p, q)) for p in range(HY)] for w in range(2) for q in range(HX)]
        ).astype(BF),
        by[...],
    )
    for q in range(HX):
        for p in range(HY):
            u, v = part(back_top, q, p), part(back_top, HX + q, p)
            back_out[pl.ds(4 * crossed(2 * q, 2 * p), 8), :] = jnp.where(left, u, swap(v)).astype(BF)
            back_out[pl.ds(4 * crossed(2 * q, 2 * p + 1), 8), :] = jnp.where(left, swap(u), v).astype(BF)
    exchange(3, back_out, crossed, back_home, me, recv_sem.at[gx // 2])

    copies[6].wait()
    copies[7].wait()
    supt[...] = jnp.transpose(sup_v[...])
    words = lax.broadcasted_iota(jnp.int32, (16, 128), 0)

    def gather_bits(i, acc):
        tile = supt[pl.ds(pl.multiple_of(i * 8, 8), 8), :]
        word = lax.shift_right_logical(tile, 5)
        bit = lax.shift_left(jnp.ones_like(tile), tile & 31)
        for n in range(8):
            hit = words == word[n : n + 1, :]
            acc = acc | jnp.where(hit, bit[n : n + 1, :], 0)
        return acc

    bits[...] = lax.fori_loop(0, 32, gather_bits, jnp.zeros((16, 128), jnp.int32))
    place = lax.broadcasted_iota(jnp.int32, (32, 128), 0)
    diagonal = lax.broadcasted_iota(jnp.int32, (16, 16), 0) == lax.broadcasted_iota(
        jnp.int32, (16, 16), 1
    )
    columns = [
        jnp.sum(jnp.where(diagonal, thr_v[l : l + 1, :], 0.0), axis=1, keepdims=True)
        for l in range(8)
    ]
    column = jnp.concatenate(columns, axis=0)
    for c in range(4):
        stacked = jnp.concatenate(
            [lax.shift_right_logical(jnp.broadcast_to(bits[4 * c + w : 4 * c + w + 1, :], (32, 128)), place) & 1
             for w in range(4)],
            axis=0,
        )
        kept = jnp.transpose(stacked.astype(F32))
        teff[:, 128 * c : 128 * c + 128] = jnp.where(kept > 0.0, column, jnp.inf)

    arrive(low_home, recv_sem.at[10])
    for w, basis in enumerate((s_lo, s_hi)):
        for b in range(4):
            block = pl.ds(512 * w + 128 * b, 128)
            predicted = dot(low_home[pl.ds(128 * b, 128), :], basis[...])
            res_v[block, :] = (s_v[block, :].astype(F32) - predicted).astype(BF)

    @pl.loop(0, 8)
    def _(i):
        z = plane(i)
        rows = pl.ds(pl.multiple_of(64 * z, 64), 64)
        arrive(back_home.at[rows], recv_sem.at[z])
        home = back_home[rows, :]
        t = teff[pl.ds(pl.multiple_of(64 * lax.rem(z, 2), 64), 64), :]
        for w, basis in enumerate((e_lo, e_hi)):
            block = pl.ds(pl.multiple_of(512 * w + 64 * z, 64), 64)
            v = m_v[block, :].astype(F32) + dot(home, basis[...])
            om_v[block, :] = v - jnp.minimum(jnp.maximum(v, -t), t)

    for i, src in enumerate((top_out, smp_out, low_out, back_out)):
        sent = src.at[pl.ds(0, 4 * (N - 1))]
        pltpu.make_async_copy(sent, sent, send_sem.at[i]).wait()


def deliver(model_v, residual_v, model_next, residual, sem):
    copies = [
        pltpu.make_async_copy(model_v, model_next, sem.at[0]),
        pltpu.make_async_copy(residual_v, residual, sem.at[1]),
    ]
    for copy in copies:
        copy.start()
    for copy in copies:
        copy.wait()


def on_device(
    samples, model_prev, threshold, support, sample_basis, eval_basis, transfer_x, transfer_y
):
    hbm = pl.BlockSpec(memory_space=pltpu.HBM)
    traffic = pltpu.VMEM((4 * N, 128), BF)
    model_next, residual = pl.pallas_call(
        kernel,
        out_shape=(
            jax.ShapeDtypeStruct((1024, 512), F32),
            jax.ShapeDtypeStruct((1024, 512), BF),
        ),
        in_specs=[hbm] * 8,
        out_specs=(pl.BlockSpec(memory_space=pltpu.VMEM),) * 2,
        scratch_shapes=[
            pltpu.VMEM((1024, 512), BF),
            pltpu.VMEM((1024, 512), BF),
            pltpu.VMEM((16, 1024, 64), BF),
            pltpu.VMEM((8, 512, 64), BF),
            pltpu.VMEM((1024, 1024), BF),
            pltpu.VMEM((512, 512), BF),
            pltpu.VMEM((64, 512), BF),
            pltpu.VMEM((64, 512), BF),
            pltpu.VMEM((128, 512), BF),
            pltpu.VMEM((128, 512), BF),
            pltpu.VMEM((128, 512), BF),
            pltpu.VMEM((128, 512), BF),
            pltpu.VMEM((256, 128), BF),
            pltpu.VMEM((128, 256), jnp.int32),
            pltpu.VMEM((256, 128), jnp.int32),
            pltpu.VMEM((16, 128), jnp.int32),
            pltpu.VMEM((8, 16), F32),
            pltpu.VMEM((128, 512), F32),
            traffic, traffic, traffic, traffic, traffic, traffic, traffic, traffic,
            pltpu.SemaphoreType.DMA((8,)),
            pltpu.SemaphoreType.DMA((4,)),
            pltpu.SemaphoreType.DMA((11,)),
        ],
        compiler_params=pltpu.CompilerParams(
            collective_id=0, has_side_effects=True, vmem_limit_bytes=30 * 2**20
        ),
    )(
        *[pltpu.with_memory_space_constraint(v, pltpu.HBM) for v in (
        samples.reshape(1024, 512),
        model_prev.reshape(1024, 512),
        threshold,
        support.reshape(128, 256),
        sample_basis.T,
        eval_basis,
        transfer_x.reshape(16, 1024, 64),
        transfer_y.reshape(8, 512, 64),
    )])
    vmem = pl.BlockSpec(memory_space=pltpu.VMEM)
    model_next, residual = pl.pallas_call(
        deliver,
        out_shape=(
            jax.ShapeDtypeStruct((1024, 512), F32),
            jax.ShapeDtypeStruct((1024, 512), BF),
        ),
        in_specs=[vmem, vmem],
        out_specs=(hbm, hbm),
        scratch_shapes=[pltpu.SemaphoreType.DMA((2,))],
        compiler_params=pltpu.CompilerParams(vmem_limit_bytes=2 * 2**20),
    )(model_next, residual)
    return model_next.reshape(8, 8, 16, 512), residual.reshape(8, 8, 16, 512)


def solution(mesh):
    return jax.shard_map(
        on_device,
        mesh=mesh,
        in_specs=(
            P("ga", "gx", "gy", None),
            P("ga", "gx", "gy", None),
            P("gx", "gy"),
            P("gx", "gy", None),
            P(),
            P(),
            P(),
            P(),
        ),
        out_specs=(P("ga", "gx", "gy", None), P("ga", "gx", "gy", None)),
        check_vma=False,
    )
```

```python
import jax
import jax.numpy as jnp
from jax import lax
from jax.experimental import pallas as pl
from jax.experimental.pallas import tpu as pltpu
from jax.sharding import PartitionSpec as P

BF = jnp.bfloat16
F32 = jnp.float32
MESH = pl.DeviceIdType.MESH
NX, NY = 16, 8
N = NX * NY
LAST = (((1,), (1,)), ((), ()))
PLAIN = (((1,), (0,)), ((), ()))


def dot(a, b, dims=PLAIN):
    return lax.dot_general(a, b, dims, preferred_element_type=F32)


def kernel(
    samples, model, thr, sup, sb, eb, tx, ty,
    om_v, res_v,
    m_v, s_v, tx_v, ty_v, bx, by, sb_v, eb_v, e_lo, s_lo, e_hi, s_hi, gram, sup_v, supt, bits, thr_v, teff,
    top_out, top_in, smp_out, smp_in, low_out, low_home, back_out, back_home,
    in_sem, send_sem, recv_sem,
):
    gx, gy = lax.axis_index("gx"), lax.axis_index("gy")
    me = gx * NY + gy
    left = lax.broadcasted_iota(jnp.int32, (8, 128), 1) < 64
    straight = left == (lax.broadcasted_iota(jnp.int32, (8, 128), 0) < 4)

    def swap(u):
        return pltpu.roll(u, 64, 1)

    def turn(u):
        return jnp.where(straight, u, pltpu.roll(swap(u), 4, 0))

    loads = [
        (model, m_v), (eb, eb_v), (sb, sb_v), (samples, s_v),
        (ty, ty_v), (tx, tx_v), (sup, sup_v), (thr, thr_v),
    ]
    copies = [
        pltpu.make_async_copy(src, dst, in_sem.at[i]) for i, (src, dst) in enumerate(loads)
    ]

    def plane(i):
        away = (i + 1) // 2
        return lax.rem(gx // 2 + 4 + jnp.where(lax.rem(i, 2) == 0, away, 8 - away), 8)

    columns_y = [lax.rem(gy + d, NY) for d in (6, 2, 5, 3, 4, 7, 1)] + [gy]

    def each_partner(act):
        @pl.loop(0, NX - 1)
        def _(i):
            away = (i + 1) // 2
            x = lax.rem(gx + 8 + jnp.where(lax.rem(i, 2) == 0, away, NX - away), NX)
            for y in columns_y:
                act(x, y)

        for y in columns_y[:-1]:
            act(gx, y)

    barrier = pltpu.get_barrier_semaphore()

    each_partner(
        lambda x, y: pl.semaphore_signal(
            barrier, inc=1, device_id={"gx": x, "gy": y}, device_id_type=MESH
        )
    )
    for copy in copies:
        copy.start()

    copies[1].wait()
    e = eb_v[...]
    zero = jnp.zeros_like(e)
    e_lo[...] = jnp.concatenate([e, zero], axis=0)
    e_hi[...] = jnp.concatenate([zero, e], axis=0)
    copies[2].wait()
    base = sb_v[...]
    s_lo[...] = jnp.concatenate([base, zero], axis=0)
    s_hi[...] = jnp.concatenate([zero, base], axis=0)
    copies[0].wait()
    top_out[...] = (dot(m_v[:512], e_lo[...], LAST) + dot(m_v[512:], e_hi[...], LAST)).astype(BF)

    pl.semaphore_wait(barrier, N - 1)

    def slot(i):
        return pl.ds(pl.multiple_of(i * 4, 4), 4)

    def along(x, y):
        return x * NY + y

    def crossed(x, y):
        return y * NX + x

    def exchange(i, src, at, dst, here, arrived):
        def send(x, y):
            pltpu.make_async_remote_copy(
                src_ref=src.at[slot(at(x, y))], dst_ref=dst.at[slot(here)],
                send_sem=send_sem.at[i], recv_sem=arrived,
                device_id={"gx": x, "gy": y}, device_id_type=MESH,
            ).start()

        each_partner(send)
        pltpu.make_async_copy(src.at[slot(at(gx, gy))], dst.at[slot(here)], arrived).start()

    def arrive(dst, arrived):
        pltpu.make_async_copy(dst, dst, arrived).wait()

    exchange(0, top_out, along, top_in, crossed(gx, gy), recv_sem.at[8])

    copies[3].wait()
    smp_out[...] = (dot(s_v[:512], s_lo[...], LAST) + dot(s_v[512:], s_hi[...], LAST)).astype(BF)
    exchange(1, smp_out, along, smp_in, me, recv_sem.at[9])

    block = dot(s_lo[...], s_lo[...], LAST) + dot(s_hi[...], s_hi[...], LAST)
    major = block.astype(BF)
    gram[:128] = major
    gram[128:] = (block - major.astype(F32)).astype(BF)

    copies[4].wait()
    for p in range(NY // 2):
        @pl.loop(0, 4)
        def _(i):
            rows = pl.ds(pl.multiple_of(128 * i, 128), 128)
            by[rows, 128 * p : 128 * p + 128] = jnp.concatenate(
                [ty_v[2 * p, rows, :], ty_v[2 * p + 1, rows, :]], axis=1
            )

    copies[5].wait()
    for p in range(NX // 2):
        @pl.loop(0, 8)
        def _(i):
            rows = pl.ds(pl.multiple_of(128 * i, 128), 128)
            bx[rows, 128 * p : 128 * p + 128] = jnp.concatenate(
                [tx_v[2 * p, rows, :], tx_v[2 * p + 1, rows, :]], axis=1
            )

    def tile(ref, i):
        return ref[pl.ds(4 * i, 8), :].astype(F32)

    def assembled(parts):
        return jnp.concatenate([jnp.concatenate(row, axis=1) for row in parts], axis=0)

    def paired(ref, i, k):
        u, v = tile(ref, i), tile(ref, k)
        return jnp.where(left, u, swap(v)), jnp.where(left, swap(u), v)

    def part(u, i, k):
        return u[8 * i : 8 * i + 8, 128 * k : 128 * k + 128]

    HX, HY = NX // 2, NY // 2
    arrive(top_in, recv_sem.at[8])
    parts = [[None] * HY for _ in range(NX)]
    for q in range(HX):
        for p in range(HY):
            parts[q][p], parts[HX + q][p] = paired(
                top_in, crossed(2 * q, 2 * p), crossed(2 * q, 2 * p + 1)
            )
    middle = dot(assembled(parts).astype(BF), by[...], LAST)
    low = dot(
        assembled(
            [[turn(part(middle, HX * w + q, p)) for q in range(HX)] for w in range(2) for p in range(HY)]
        ).astype(BF),
        bx[...],
        LAST,
    )
    for q in range(HX):
        for p in range(HY):
            u, v = part(low, p, q), part(low, HY + p, q)
            low_out[pl.ds(4 * along(2 * q, 2 * p), 8), :] = jnp.where(left, u, swap(v)).astype(BF)
            low_out[pl.ds(4 * along(2 * q + 1, 2 * p), 8), :] = jnp.where(left, swap(u), v).astype(BF)
    exchange(2, low_out, along, low_home, me, recv_sem.at[10])

    low_bf = low.astype(BF)
    stacked = jnp.concatenate([low_bf[:, 128 * q : 128 * q + 128] for q in range(HX)], axis=0)
    taken = dot(stacked, gram[:128]) + dot(stacked, gram[128:])
    arrive(smp_in, recv_sem.at[9])
    parts = [[None] * HX for _ in range(NY)]
    for q in range(HX):
        for p in range(HY):
            u, v = paired(smp_in, along(2 * q, 2 * p), along(2 * q + 1, 2 * p))
            parts[p][q] = u - part(taken, NY * q + p, 0)
            parts[HY + p][q] = v - part(taken, NY * q + HY + p, 0)
    back_mid = dot(assembled(parts).astype(BF), bx[...])
    back_top = dot(
        assembled(
            [[turn(part(back_mid, HY * w + p, q)) for p in range(HY)] for w in range(2) for q in range(HX)]
        ).astype(BF),
        by[...],
    )
    for q in range(HX):
        for p in range(HY):
            u, v = part(back_top, q, p), part(back_top, HX + q, p)
            back_out[pl.ds(4 * crossed(2 * q, 2 * p), 8), :] = jnp.where(left, u, swap(v)).astype(BF)
            back_out[pl.ds(4 * crossed(2 * q, 2 * p + 1), 8), :] = jnp.where(left, swap(u), v).astype(BF)
    exchange(3, back_out, crossed, back_home, me, recv_sem.at[gx // 2])

    copies[6].wait()
    copies[7].wait()
    supt[...] = jnp.transpose(sup_v[...])
    words = lax.broadcasted_iota(jnp.int32, (16, 128), 0)

    def gather_bits(i, acc):
        tile = supt[pl.ds(pl.multiple_of(i * 8, 8), 8), :]
        word = lax.shift_right_logical(tile, 5)
        bit = lax.shift_left(jnp.ones_like(tile), tile & 31)
        for n in range(8):
            hit = words == word[n : n + 1, :]
            acc = acc | jnp.where(hit, bit[n : n + 1, :], 0)
        return acc

    bits[...] = lax.fori_loop(0, 32, gather_bits, jnp.zeros((16, 128), jnp.int32))
    place = lax.broadcasted_iota(jnp.int32, (32, 128), 0)
    diagonal = lax.broadcasted_iota(jnp.int32, (16, 16), 0) == lax.broadcasted_iota(
        jnp.int32, (16, 16), 1
    )
    columns = [
        jnp.sum(jnp.where(diagonal, thr_v[l : l + 1, :], 0.0), axis=1, keepdims=True)
        for l in range(8)
    ]
    column = jnp.concatenate(columns, axis=0)
    for c in range(4):
        stacked = jnp.concatenate(
            [lax.shift_right_logical(jnp.broadcast_to(bits[4 * c + w : 4 * c + w + 1, :], (32, 128)), place) & 1
             for w in range(4)],
            axis=0,
        )
        kept = jnp.transpose(stacked.astype(F32))
        teff[:, 128 * c : 128 * c + 128] = jnp.where(kept > 0.0, column, jnp.inf)

    arrive(low_home, recv_sem.at[10])
    @pl.loop(0, 4)
    def _(b):
        home = low_home[pl.ds(pl.multiple_of(128 * b, 128), 128), :]
        for w, basis in enumerate((s_lo, s_hi)):
            block = pl.ds(pl.multiple_of(512 * w + 128 * b, 128), 128)
            res_v[block, :] = (s_v[block, :].astype(F32) - dot(home, basis[...])).astype(BF)

    @pl.loop(0, 2)
    def _(i):
        zs = [plane(i * 4 + k) for k in range(4)]
        for z in zs:
            arrive(back_home.at[pl.ds(pl.multiple_of(64 * z, 64), 64)], recv_sem.at[z])
        home = jnp.concatenate(
            [back_home[pl.ds(pl.multiple_of(64 * z, 64), 64), :] for z in zs], axis=0
        )
        for w, basis in enumerate((e_lo, e_hi)):
            update = dot(home, basis[...])
            for k, z in enumerate(zs):
                block = pl.ds(pl.multiple_of(512 * w + 64 * z, 64), 64)
                t = teff[pl.ds(pl.multiple_of(64 * lax.rem(z, 2), 64), 64), :]
                v = m_v[block, :].astype(F32) + update[64 * k : 64 * k + 64]
                om_v[block, :] = v - jnp.minimum(jnp.maximum(v, -t), t)

    for i, src in enumerate((top_out, smp_out, low_out, back_out)):
        sent = src.at[pl.ds(0, 4 * (N - 1))]
        pltpu.make_async_copy(sent, sent, send_sem.at[i]).wait()


def deliver(model_v, residual_v, model_next, residual, sem):
    copies = [
        pltpu.make_async_copy(model_v, model_next, sem.at[0]),
        pltpu.make_async_copy(residual_v, residual, sem.at[1]),
    ]
    for copy in copies:
        copy.start()
    for copy in copies:
        copy.wait()


def on_device(
    samples, model_prev, threshold, support, sample_basis, eval_basis, transfer_x, transfer_y
):
    hbm = pl.BlockSpec(memory_space=pltpu.HBM)
    traffic = pltpu.VMEM((4 * N, 128), BF)
    model_next, residual = pl.pallas_call(
        kernel,
        out_shape=(
            jax.ShapeDtypeStruct((1024, 512), F32),
            jax.ShapeDtypeStruct((1024, 512), BF),
        ),
        in_specs=[hbm] * 8,
        out_specs=(pl.BlockSpec(memory_space=pltpu.VMEM),) * 2,
        scratch_shapes=[
            pltpu.VMEM((1024, 512), BF),
            pltpu.VMEM((1024, 512), BF),
            pltpu.VMEM((16, 1024, 64), BF),
            pltpu.VMEM((8, 512, 64), BF),
            pltpu.VMEM((1024, 1024), BF),
            pltpu.VMEM((512, 512), BF),
            pltpu.VMEM((64, 512), BF),
            pltpu.VMEM((64, 512), BF),
            pltpu.VMEM((128, 512), BF),
            pltpu.VMEM((128, 512), BF),
            pltpu.VMEM((128, 512), BF),
            pltpu.VMEM((128, 512), BF),
            pltpu.VMEM((256, 128), BF),
            pltpu.VMEM((128, 256), jnp.int32),
            pltpu.VMEM((256, 128), jnp.int32),
            pltpu.VMEM((16, 128), jnp.int32),
            pltpu.VMEM((8, 16), F32),
            pltpu.VMEM((128, 512), F32),
            traffic, traffic, traffic, traffic, traffic, traffic, traffic, traffic,
            pltpu.SemaphoreType.DMA((8,)),
            pltpu.SemaphoreType.DMA((4,)),
            pltpu.SemaphoreType.DMA((11,)),
        ],
        compiler_params=pltpu.CompilerParams(
            collective_id=0, has_side_effects=True, vmem_limit_bytes=30 * 2**20
        ),
    )(
        *[pltpu.with_memory_space_constraint(v, pltpu.HBM) for v in (
        samples.reshape(1024, 512),
        model_prev.reshape(1024, 512),
        threshold,
        support.reshape(128, 256),
        sample_basis.T,
        eval_basis,
        transfer_x.reshape(16, 1024, 64),
        transfer_y.reshape(8, 512, 64),
    )])
    vmem = pl.BlockSpec(memory_space=pltpu.VMEM)
    model_next, residual = pl.pallas_call(
        deliver,
        out_shape=(
            jax.ShapeDtypeStruct((1024, 512), F32),
            jax.ShapeDtypeStruct((1024, 512), BF),
        ),
        in_specs=[vmem, vmem],
        out_specs=(hbm, hbm),
        scratch_shapes=[pltpu.SemaphoreType.DMA((2,))],
        compiler_params=pltpu.CompilerParams(vmem_limit_bytes=2 * 2**20),
    )(model_next, residual)
    return model_next.reshape(8, 8, 16, 512), residual.reshape(8, 8, 16, 512)


def solution(mesh):
    return jax.shard_map(
        on_device,
        mesh=mesh,
        in_specs=(
            P("ga", "gx", "gy", None),
            P("ga", "gx", "gy", None),
            P("gx", "gy"),
            P("gx", "gy", None),
            P(),
            P(),
            P(),
            P(),
        ),
        out_specs=(P("ga", "gx", "gy", None), P("ga", "gx", "gy", None)),
        check_vma=False,
    )
```

```python
import jax
import jax.numpy as jnp
from jax import lax
from jax.experimental import pallas as pl
from jax.experimental.pallas import tpu as pltpu
from jax.sharding import PartitionSpec as P

BF = jnp.bfloat16
F32 = jnp.float32
MESH = pl.DeviceIdType.MESH
NX, NY = 16, 8
N = NX * NY
LAST = (((1,), (1,)), ((), ()))
PLAIN = (((1,), (0,)), ((), ()))


def dot(a, b, dims=PLAIN):
    return lax.dot_general(a, b, dims, preferred_element_type=F32)


def kernel(
    samples, model, thr, sup, sb, eb, tx, ty,
    om_v, res_v,
    m_v, s_v, tx_v, ty_v, bx, by, sb_v, eb_v, e_lo, s_lo, e_hi, s_hi, gram, sup_v, supt, bits, thr_v, teff,
    top_out, top_in, smp_out, smp_in, low_out, low_home, back_out, back_home,
    in_sem, send_sem, recv_sem,
):
    gx, gy = lax.axis_index("gx"), lax.axis_index("gy")
    me = gx * NY + gy
    left = lax.broadcasted_iota(jnp.int32, (8, 128), 1) < 64
    straight = left == (lax.broadcasted_iota(jnp.int32, (8, 128), 0) < 4)

    def swap(u):
        return pltpu.roll(u, 64, 1)

    def turn(u):
        return jnp.where(straight, u, pltpu.roll(swap(u), 4, 0))

    loads = [
        (model, m_v), (eb, eb_v), (sb, sb_v), (samples, s_v),
        (ty, ty_v), (tx, tx_v), (sup, sup_v), (thr, thr_v),
    ]
    copies = [
        pltpu.make_async_copy(src, dst, in_sem.at[i]) for i, (src, dst) in enumerate(loads)
    ]

    def plane(i):
        away = (i + 1) // 2
        return lax.rem(gx // 2 + 4 + jnp.where(lax.rem(i, 2) == 0, away, 8 - away), 8)

    columns_y = [lax.rem(gy + d, NY) for d in (6, 2, 5, 3, 4, 7, 1)] + [gy]

    def each_partner(act):
        @pl.loop(0, NX - 1)
        def _(i):
            away = (i + 1) // 2
            x = lax.rem(gx + 8 + jnp.where(lax.rem(i, 2) == 0, away, NX - away), NX)
            for y in columns_y:
                act(x, y)

        for y in columns_y[:-1]:
            act(gx, y)

    def each_below(ys, act):
        @pl.loop(0, NX - 1)
        def _(i):
            away = (i + 1) // 2
            x = lax.rem(gx + 8 + jnp.where(lax.rem(i, 2) == 0, away, NX - away), NX)
            for y in ys:
                act(x, y)

        for y in ys:
            @pl.when(y != gy)
            def _():
                act(gx, y)

    barrier = pltpu.get_barrier_semaphore()

    each_partner(
        lambda x, y: pl.semaphore_signal(
            barrier, inc=1, device_id={"gx": x, "gy": y}, device_id_type=MESH
        )
    )
    for copy in copies:
        copy.start()

    copies[1].wait()
    e = eb_v[...]
    zero = jnp.zeros_like(e)
    e_lo[...] = jnp.concatenate([e, zero], axis=0)
    e_hi[...] = jnp.concatenate([zero, e], axis=0)
    copies[2].wait()
    base = sb_v[...]
    s_lo[...] = jnp.concatenate([base, zero], axis=0)
    s_hi[...] = jnp.concatenate([zero, base], axis=0)
    copies[0].wait()
    top_out[...] = (dot(m_v[:512], e_lo[...], LAST) + dot(m_v[512:], e_hi[...], LAST)).astype(BF)

    pl.semaphore_wait(barrier, N - 1)

    def slot(i):
        return pl.ds(pl.multiple_of(i * 4, 4), 4)

    def along(x, y):
        return x * NY + y

    def crossed(x, y):
        return y * NX + x

    def exchange(i, src, at, dst, here, arrived):
        def send(x, y):
            pltpu.make_async_remote_copy(
                src_ref=src.at[slot(at(x, y))], dst_ref=dst.at[slot(here)],
                send_sem=send_sem.at[i], recv_sem=arrived,
                device_id={"gx": x, "gy": y}, device_id_type=MESH,
            ).start()

        each_partner(send)
        pltpu.make_async_copy(src.at[slot(at(gx, gy))], dst.at[slot(here)], arrived).start()

    def arrive(dst, arrived):
        pltpu.make_async_copy(dst, dst, arrived).wait()

    exchange(0, top_out, along, top_in, crossed(gx, gy), recv_sem.at[8])

    copies[3].wait()
    smp_out[...] = (dot(s_v[:512], s_lo[...], LAST) + dot(s_v[512:], s_hi[...], LAST)).astype(BF)
    exchange(1, smp_out, along, smp_in, me, recv_sem.at[9])

    block = dot(s_lo[...], s_lo[...], LAST) + dot(s_hi[...], s_hi[...], LAST)
    major = block.astype(BF)
    gram[:128] = major
    gram[128:] = (block - major.astype(F32)).astype(BF)

    copies[4].wait()
    for p in range(NY // 2):
        @pl.loop(0, 4)
        def _(i):
            rows = pl.ds(pl.multiple_of(128 * i, 128), 128)
            by[rows, 128 * p : 128 * p + 128] = jnp.concatenate(
                [ty_v[2 * p, rows, :], ty_v[2 * p + 1, rows, :]], axis=1
            )

    copies[5].wait()
    for p in range(NX // 2):
        @pl.loop(0, 8)
        def _(i):
            rows = pl.ds(pl.multiple_of(128 * i, 128), 128)
            bx[rows, 128 * p : 128 * p + 128] = jnp.concatenate(
                [tx_v[2 * p, rows, :], tx_v[2 * p + 1, rows, :]], axis=1
            )

    def tile(ref, i):
        return ref[pl.ds(4 * i, 8), :].astype(F32)

    def assembled(parts):
        return jnp.concatenate([jnp.concatenate(row, axis=1) for row in parts], axis=0)

    def paired(ref, i, k):
        u, v = tile(ref, i), tile(ref, k)
        return jnp.where(left, u, swap(v)), jnp.where(left, swap(u), v)

    def part(u, i, k):
        return u[8 * i : 8 * i + 8, 128 * k : 128 * k + 128]

    HX, HY = NX // 2, NY // 2
    arrive(top_in, recv_sem.at[8])
    parts = [[None] * HY for _ in range(NX)]
    for q in range(HX):
        for p in range(HY):
            parts[q][p], parts[HX + q][p] = paired(
                top_in, crossed(2 * q, 2 * p), crossed(2 * q, 2 * p + 1)
            )
    middle = dot(assembled(parts).astype(BF), by[...], LAST)
    low = dot(
        assembled(
            [[turn(part(middle, HX * w + q, p)) for q in range(HX)] for w in range(2) for p in range(HY)]
        ).astype(BF),
        bx[...],
        LAST,
    )
    for q in range(HX):
        for p in range(HY):
            u, v = part(low, p, q), part(low, HY + p, q)
            low_out[pl.ds(4 * along(2 * q, 2 * p), 8), :] = jnp.where(left, u, swap(v)).astype(BF)
            low_out[pl.ds(4 * along(2 * q + 1, 2 * p), 8), :] = jnp.where(left, swap(u), v).astype(BF)
    exchange(2, low_out, along, low_home, me, recv_sem.at[10])

    low_bf = low.astype(BF)
    stacked = jnp.concatenate([low_bf[:, 128 * q : 128 * q + 128] for q in range(HX)], axis=0)
    taken = dot(stacked, gram[:128]) + dot(stacked, gram[128:])
    arrive(smp_in, recv_sem.at[9])
    parts = [[None] * HX for _ in range(NY)]
    for q in range(HX):
        for p in range(HY):
            u, v = paired(smp_in, along(2 * q, 2 * p), along(2 * q + 1, 2 * p))
            parts[p][q] = u - part(taken, NY * q + p, 0)
            parts[HY + p][q] = v - part(taken, NY * q + HY + p, 0)
    back_mid = dot(assembled(parts).astype(BF), bx[...])
    turned = assembled(
        [[turn(part(back_mid, HY * w + p, q)) for p in range(HY)] for w in range(2) for q in range(HX)]
    ).astype(BF)

    def send_back(x, y):
        pltpu.make_async_remote_copy(
            src_ref=back_out.at[slot(crossed(x, y))], dst_ref=back_home.at[slot(me)],
            send_sem=send_sem.at[3], recv_sem=recv_sem.at[gx // 2],
            device_id={"gx": x, "gy": y}, device_id_type=MESH,
        ).start()

    for near in (0, 2):
        back_top = dot(turned, by[:, 128 * near : 128 * near + 256])
        for q in range(HX):
            for p in range(2):
                u, v = part(back_top, q, p), part(back_top, HX + q, p)
                y = 2 * (near + p)
                back_out[pl.ds(4 * crossed(2 * q, y), 8), :] = jnp.where(left, u, swap(v)).astype(BF)
                back_out[pl.ds(4 * crossed(2 * q, y + 1), 8), :] = jnp.where(left, swap(u), v).astype(BF)
        each_below(range(2 * near, 2 * near + 4), send_back)
    pltpu.make_async_copy(
        back_out.at[slot(crossed(gx, gy))], back_home.at[slot(me)], recv_sem.at[gx // 2]
    ).start()

    copies[6].wait()
    copies[7].wait()
    supt[...] = jnp.transpose(sup_v[...])
    words = lax.broadcasted_iota(jnp.int32, (16, 128), 0)

    def gather_bits(i, acc):
        tile = supt[pl.ds(pl.multiple_of(i * 8, 8), 8), :]
        word = lax.shift_right_logical(tile, 5)
        bit = lax.shift_left(jnp.ones_like(tile), tile & 31)
        for n in range(8):
            hit = words == word[n : n + 1, :]
            acc = acc | jnp.where(hit, bit[n : n + 1, :], 0)
        return acc

    bits[...] = lax.fori_loop(0, 32, gather_bits, jnp.zeros((16, 128), jnp.int32))
    place = lax.broadcasted_iota(jnp.int32, (32, 128), 0)
    diagonal = lax.broadcasted_iota(jnp.int32, (16, 16), 0) == lax.broadcasted_iota(
        jnp.int32, (16, 16), 1
    )
    columns = [
        jnp.sum(jnp.where(diagonal, thr_v[l : l + 1, :], 0.0), axis=1, keepdims=True)
        for l in range(8)
    ]
    column = jnp.concatenate(columns, axis=0)
    for c in range(4):
        stacked = jnp.concatenate(
            [lax.shift_right_logical(jnp.broadcast_to(bits[4 * c + w : 4 * c + w + 1, :], (32, 128)), place) & 1
             for w in range(4)],
            axis=0,
        )
        kept = jnp.transpose(stacked.astype(F32))
        teff[:, 128 * c : 128 * c + 128] = jnp.where(kept > 0.0, column, jnp.inf)

    arrive(low_home, recv_sem.at[10])
    @pl.loop(0, 4)
    def _(b):
        home = low_home[pl.ds(pl.multiple_of(128 * b, 128), 128), :]
        for w, basis in enumerate((s_lo, s_hi)):
            block = pl.ds(pl.multiple_of(512 * w + 128 * b, 128), 128)
            res_v[block, :] = (s_v[block, :].astype(F32) - dot(home, basis[...])).astype(BF)

    @pl.loop(0, 2)
    def _(i):
        zs = [plane(i * 4 + k) for k in range(4)]
        for z in zs:
            arrive(back_home.at[pl.ds(pl.multiple_of(64 * z, 64), 64)], recv_sem.at[z])
        home = jnp.concatenate(
            [back_home[pl.ds(pl.multiple_of(64 * z, 64), 64), :] for z in zs], axis=0
        )
        for w, basis in enumerate((e_lo, e_hi)):
            update = dot(home, basis[...])
            for k, z in enumerate(zs):
                block = pl.ds(pl.multiple_of(512 * w + 64 * z, 64), 64)
                t = teff[pl.ds(pl.multiple_of(64 * lax.rem(z, 2), 64), 64), :]
                v = m_v[block, :].astype(F32) + update[64 * k : 64 * k + 64]
                om_v[block, :] = v - jnp.minimum(jnp.maximum(v, -t), t)

    for i, src in enumerate((top_out, smp_out, low_out, back_out)):
        sent = src.at[pl.ds(0, 4 * (N - 1))]
        pltpu.make_async_copy(sent, sent, send_sem.at[i]).wait()


def deliver(model_v, residual_v, model_next, residual, sem):
    copies = [
        pltpu.make_async_copy(model_v, model_next, sem.at[0]),
        pltpu.make_async_copy(residual_v, residual, sem.at[1]),
    ]
    for copy in copies:
        copy.start()
    for copy in copies:
        copy.wait()


def on_device(
    samples, model_prev, threshold, support, sample_basis, eval_basis, transfer_x, transfer_y
):
    hbm = pl.BlockSpec(memory_space=pltpu.HBM)
    traffic = pltpu.VMEM((4 * N, 128), BF)
    model_next, residual = pl.pallas_call(
        kernel,
        out_shape=(
            jax.ShapeDtypeStruct((1024, 512), F32),
            jax.ShapeDtypeStruct((1024, 512), BF),
        ),
        in_specs=[hbm] * 8,
        out_specs=(pl.BlockSpec(memory_space=pltpu.VMEM),) * 2,
        scratch_shapes=[
            pltpu.VMEM((1024, 512), BF),
            pltpu.VMEM((1024, 512), BF),
            pltpu.VMEM((16, 1024, 64), BF),
            pltpu.VMEM((8, 512, 64), BF),
            pltpu.VMEM((1024, 1024), BF),
            pltpu.VMEM((512, 512), BF),
            pltpu.VMEM((64, 512), BF),
            pltpu.VMEM((64, 512), BF),
            pltpu.VMEM((128, 512), BF),
            pltpu.VMEM((128, 512), BF),
            pltpu.VMEM((128, 512), BF),
            pltpu.VMEM((128, 512), BF),
            pltpu.VMEM((256, 128), BF),
            pltpu.VMEM((128, 256), jnp.int32),
            pltpu.VMEM((256, 128), jnp.int32),
            pltpu.VMEM((16, 128), jnp.int32),
            pltpu.VMEM((8, 16), F32),
            pltpu.VMEM((128, 512), F32),
            traffic, traffic, traffic, traffic, traffic, traffic, traffic, traffic,
            pltpu.SemaphoreType.DMA((8,)),
            pltpu.SemaphoreType.DMA((4,)),
            pltpu.SemaphoreType.DMA((11,)),
        ],
        compiler_params=pltpu.CompilerParams(
            collective_id=0, has_side_effects=True, vmem_limit_bytes=30 * 2**20
        ),
    )(
        *[pltpu.with_memory_space_constraint(v, pltpu.HBM) for v in (
        samples.reshape(1024, 512),
        model_prev.reshape(1024, 512),
        threshold,
        support.reshape(128, 256),
        sample_basis.T,
        eval_basis,
        transfer_x.reshape(16, 1024, 64),
        transfer_y.reshape(8, 512, 64),
    )])
    vmem = pl.BlockSpec(memory_space=pltpu.VMEM)
    model_next, residual = pl.pallas_call(
        deliver,
        out_shape=(
            jax.ShapeDtypeStruct((1024, 512), F32),
            jax.ShapeDtypeStruct((1024, 512), BF),
        ),
        in_specs=[vmem, vmem],
        out_specs=(hbm, hbm),
        scratch_shapes=[pltpu.SemaphoreType.DMA((2,))],
        compiler_params=pltpu.CompilerParams(vmem_limit_bytes=2 * 2**20),
    )(model_next, residual)
    return model_next.reshape(8, 8, 16, 512), residual.reshape(8, 8, 16, 512)


def solution(mesh):
    return jax.shard_map(
        on_device,
        mesh=mesh,
        in_specs=(
            P("ga", "gx", "gy", None),
            P("ga", "gx", "gy", None),
            P("gx", "gy"),
            P("gx", "gy", None),
            P(),
            P(),
            P(),
            P(),
        ),
        out_specs=(P("ga", "gx", "gy", None), P("ga", "gx", "gy", None)),
        check_vma=False,
    )
```
